32 devices in a mesh: ctx: 8 (over z, x), tp: 4 (over y, core).
Axes of the slice: x: 2, y: 2, z: 4, core: 2. Of those that a mesh axis runs over, the one named last changes fastest.
Arguments:
- hidden_input: bfloat16 [256, 8192], P(None, 'ctx'), may hold values from -6 to 6
- w_query: bfloat16 [8192, 8192], P('ctx', 'tp')
- key_value_weight: bfloat16 [8192, 2, 1024], P('ctx', None, 'tp'), may hold values from -0.0625 to 0.0625
- w_out: bfloat16 [8192, 8192], P('tp', 'ctx'), may hold values from -0.0625 to 0.0625
- key_value_cache: bfloat16 [2, 8, 32768, 128], P(None, 'tp', 'ctx'), may hold values from -6 to 6
- filled: int32 [8], P('ctx'), may hold values from 512 to 4096, as said below
- positions: int32 [256], replicated, may hold values from 0 to 255, each once
Outputs:
- layer_out: bfloat16 [256, 8192], P('tp', 'ctx')
The draws below stay inside these ranges and needn't reach their ends.
Inputs may be any that keep to these rules, and one draw needn't show every extreme that they name: `filled`: every shard has at least 512 used slots; some shard is full and some holds exactly 512.
All inputs are finite; a program needn't handle non-finite values.
Results may differ from the reference program's by a relative error of at most 0.0045.
The reference program's roundings to bfloat16 on the way count: a program that leaves them out, or rounds other values in their place, can miss the bound.
Values may be sent and summed in bfloat16 or wider, within the bound.
A program may use at most 128 MiB of HBM per device.

```python
import math
import jax
import jax.numpy as jnp
from jax import lax

MODEL_WIDTH = 8192
HQ = 64
KEY_HEADS = 8
HEAD_SIZE = 128
QUERY_GROUP = 8
NEW_TOKENS = 256
S_DEV = 4096
SHARDS = 8
CACHE_SLOTS = 32768


def draw_filled(key, part):
    amounts = jax.random.randint(jax.random.fold_in(key, 11), (SHARDS,), S_DEV // 8, S_DEV + 1, dtype=jnp.int32)
    shuffled = jax.random.permutation(jax.random.fold_in(key, 12), SHARDS)
    amounts = amounts.at[shuffled[0]].set(S_DEV)
    amounts = amounts.at[shuffled[1]].set(S_DEV // 8)
    return amounts.astype(jnp.int32)


def draw_w_query(key, part):
    entry_key = jax.random.fold_in(key, 21)
    entries = jnp.clip(jax.random.normal(entry_key, (MODEL_WIDTH, HQ, HEAD_SIZE), jnp.float32), -6.0, 6.0)
    strengths = jnp.array([20.0, 40.0, 70.0], jnp.float32)
    chosen = jax.random.permutation(jax.random.fold_in(key, 22), HQ)[:3]
    head_scales = jnp.ones((HQ,), jnp.float32).at[chosen].set(strengths)
    scaled = entries * head_scales[None, :, None] * (1.0 / math.sqrt(MODEL_WIDTH))
    return scaled.reshape(MODEL_WIDTH, HQ * HEAD_SIZE).astype(jnp.bfloat16)


def levels(key, dims, cuts, low, top_value):
    def one(position, parts):
        heights = jax.random.uniform(jax.random.fold_in(jax.random.fold_in(key, 6), position), (parts,), jnp.float32, low / len(cuts), top_value / len(cuts))
        return jnp.repeat(jnp.exp(heights), dims[position] // parts).reshape((-1,) + (1,) * (len(dims) - position - 1))

    level = one(*cuts[0])
    for cut in cuts[1:]:
        level = level * one(*cut)
    return level


def gaussian(rng, dims, deviation, limit, cuts=(), held_as=jnp.bfloat16):
    values = deviation * jax.random.normal(rng, dims, jnp.float32)
    if cuts:
        values = values * levels(rng, dims, cuts, -0.22, 0.18)
    return jnp.clip(values, -limit, limit).astype(held_as)


def setup_inputs(seed: int = 0) -> dict:
    keys = jax.random.split(jax.random.key(seed), 8)
    return {
        "hidden_input": gaussian(keys[0], (NEW_TOKENS, MODEL_WIDTH), 1.0, 6.0, ((1, 8),)),
        "w_query": draw_w_query(jax.random.fold_in(keys[7], 71), 0),
        "key_value_weight": gaussian(keys[2], (MODEL_WIDTH, 2, KEY_HEADS * HEAD_SIZE), MODEL_WIDTH ** -0.5, 0.0625, ((0, 8), (2, 4))),
        "w_out": gaussian(keys[3], (HQ * HEAD_SIZE, MODEL_WIDTH), (HQ * HEAD_SIZE) ** -0.5, 0.0625, ((0, 4), (1, 8))),
        "key_value_cache": gaussian(keys[4], (2, KEY_HEADS, CACHE_SLOTS, HEAD_SIZE), 1.0, 6.0, ((1, 4), (2, 8))),
        "filled": draw_filled(jax.random.fold_in(keys[7], 71), 0),
        "positions": jax.random.permutation(keys[6], NEW_TOKENS).astype(jnp.int32),
    }


NEG_FILL = -1e+30

def attend(query_rows, key_rows, val_rows, visible):
    scores = jnp.einsum('grd,sd->grs', query_rows.astype(jnp.float32), key_rows.astype(jnp.float32)) / math.sqrt(HEAD_SIZE)
    scores = jnp.where(visible, scores, NEG_FILL)
    row_max = lax.optimization_barrier(jnp.max(scores, axis=-1))
    probs = jnp.exp(scores - row_max[..., None])
    denom = lax.optimization_barrier(jnp.sum(probs, axis=-1))
    probs_low = probs.astype(jnp.bfloat16)
    output = jnp.einsum('grs,sd->grd', probs_low.astype(jnp.float32), val_rows.astype(jnp.float32)) / denom[..., None]
    return (row_max + jnp.log(denom), output)

def reference(hidden_input, w_query, key_value_weight, w_out, key_value_cache, filled, positions):
    query_rows = jnp.dot(hidden_input, w_query, preferred_element_type=jnp.float32).astype(jnp.bfloat16)
    query_rows = query_rows.reshape(NEW_TOKENS, KEY_HEADS, QUERY_GROUP, HEAD_SIZE)
    key_value_rows = jnp.dot(hidden_input, key_value_weight.reshape(MODEL_WIDTH, 2 * KEY_HEADS * HEAD_SIZE), preferred_element_type=jnp.float32).astype(jnp.bfloat16)
    key_value_rows = key_value_rows.reshape(NEW_TOKENS, 2, KEY_HEADS, HEAD_SIZE)
    causal_mask = positions[None, :] <= positions[:, None]

    def head_results(group):
        head_queries = jnp.transpose(query_rows[:, group], (1, 0, 2))
        key_all = key_value_cache[0][group]
        val_all = key_value_cache[1][group]

        def per_shard(shard):
            begin = (shard * S_DEV).astype(jnp.int32)
            key_rows = lax.dynamic_slice_in_dim(key_all, begin, S_DEV, 0)
            val_rows = lax.dynamic_slice_in_dim(val_all, begin, S_DEV, 0)
            visible = jnp.arange(S_DEV, dtype=jnp.int32) < filled[shard]
            return attend(head_queries, key_rows, val_rows, visible[None, None, :])
        log_sums, outputs = lax.map(per_shard, jnp.arange(SHARDS, dtype=jnp.int32))
        new_log, new_out = attend(head_queries, key_value_rows[:, 0, group], key_value_rows[:, 1, group], causal_mask[None])
        all_log = jnp.concatenate([log_sums, new_log[None]], axis=0)
        all_out = jnp.concatenate([outputs, new_out[None]], axis=0)
        top_log = lax.optimization_barrier(jnp.max(all_log, axis=0))
        shares = jnp.exp(all_log - top_log[None])
        merged = lax.optimization_barrier(jnp.sum(shares[..., None] * all_out, axis=0)) / lax.optimization_barrier(jnp.sum(shares, axis=0))[..., None]
        return merged.astype(jnp.bfloat16)
    head_output = lax.map(head_results, jnp.arange(KEY_HEADS, dtype=jnp.int32))
    attended = jnp.transpose(head_output, (2, 0, 1, 3)).reshape(NEW_TOKENS, HQ * HEAD_SIZE)
    return jnp.dot(attended, w_out, preferred_element_type=jnp.float32).astype(jnp.bfloat16)
```

```python
import functools
import math

import jax
import jax.numpy as jnp
from jax import lax
from jax.experimental import pallas as pl
from jax.experimental.pallas import tpu as pltpu
from jax.sharding import PartitionSpec as P

MESH = pl.DeviceIdType.MESH
HIDE = -1e30
LOG2E = 1.4426950408889634
CORES = 2

AHEAD = 2
FRONT = 4
REAR = 2
PREP = 1
KV_SHIP = (1, 5)
LAG_Z = 2
LAG_ZG = 2
LAG_XG = 2
LAG_XO = 2
LAG_ZO = 2
LAG_ZA = 2
LAG_XA = 2
KV_X = (2, 8)
KV_Z = (5, 11)


def factor(shards):
    for inner in (8, 2) if shards > 8 else (2,):
        if shards % inner == 0:
            return shards // inner, inner
    return shards, 1


def peers_of(outer, inner):
    me = lax.axis_index("ctx")
    z = me // inner
    x = me % inner
    xs = [(x + d) % inner for d in range(1, inner)]
    zs = [(z + d) % outer for d in range(1, outer)]
    x_ids = [{"ctx": z * inner + v} for v in xs]
    z_ids = [{"ctx": v * inner + x} for v in zs]
    return x, z, xs, zs, x_ids, z_ids


def remote(src, dst, sems, place, peer):
    return pltpu.make_async_remote_copy(
        src_ref=src,
        dst_ref=dst,
        send_sem=sems[0].at[place],
        recv_sem=sems[1].at[place],
        device_id=peer,
        device_id_type=MESH,
    )


NT = (((1,), (1,)), ((), ()))


def layer_kernel(
    outer, inner, tp_size, kv_heads, dim, scale, kb,
    filled_ref, hid_ref, posq_ref, wq_ref, wkv_ref, cache_ref, wo_ref,
    out_ref,
    hid, w_buf, w_kv, k_aug, v_raw, v_aug, wo_buf,
    part_x, recv_x, acc, recv_z, part_kv, recv_kv, acc_kv, recv_kvz, k_fresh, v_fresh, q_buf,
    o_buf, lse, o_recv, lse_recv, mid, mid_lse, mid_recv, mid_lse_recv, att,
    part, core_part, core_recv, part_low, recv_t, places_ref, hidden_new,
    h_sem, w_sem, k_sem, v_sem, wo_sem,
    s1, r1, s2, r2, s3, r3, s4, r4, s5, r5, s6, r6, s7, r7, s8, r8, s9, r9, sa, ra,
    sk, rk, sj, rj, sc, rc, st, rt,
):
    heads = q_buf.shape[2]
    group = heads // kv_heads
    rows = acc.shape[2]
    half = outer * rows
    tokens = inner * half
    slots = v_raw.shape[1]
    x, z, xs, zs, x_ids, z_ids = peers_of(outer, inner)
    tp = lax.axis_index("tp")
    core = tp % CORES
    row = tp // CORES
    others = tp_size // CORES
    ys = [(row + d) % others for d in range(1, others)]
    y_ids = [{"tp": v * CORES + core} for v in ys]
    twin = {"tp": row * CORES + 1 - core}

    h_load = pltpu.make_async_copy(hid_ref, hid, h_sem)
    q_loads = [pltpu.make_async_copy(
        wq_ref.at[:, pl.ds(p * heads * dim // 2, heads * dim // 2)],
        w_buf.at[:, pl.ds(p * heads * dim // 2, heads * dim // 2)], w_sem.at[p]) for p in range(2)]
    kv_load = pltpu.make_async_copy(wkv_ref, w_kv, w_sem.at[2])
    k_loads = [
        pltpu.make_async_copy(cache_ref.at[0, g], k_aug.at[g, :, pl.ds(0, dim)], k_sem.at[g])
        for g in range(kv_heads)
    ]
    v_loads = [
        pltpu.make_async_copy(cache_ref.at[1, g], v_raw.at[g], v_sem.at[g])
        for g in range(kv_heads)
    ]
    wo_load = pltpu.make_async_copy(wo_ref, wo_buf, wo_sem)
    barrier = pltpu.get_barrier_semaphore()
    friends = x_ids + z_ids + y_ids + [twin]
    for peer in friends:
        pl.semaphore_signal(barrier, inc=1, device_id=peer, device_id_type=MESH)
    for load in [h_load] + q_loads + [kv_load] + k_loads + v_loads + [wo_load]:
        load.start()
    h_load.wait()
    q_loads[0].wait()
    pl.semaphore_wait(barrier, len(friends))

    def span(i, size):
        return pl.ds(i, size)

    def x1(i, size):
        return [remote(part_x.at[d, span(i, size)], recv_x.at[d, span(i, size)], (s1, r1), (i, d), p)
                for d, p in enumerate(x_ids)]

    def z1(i, size):
        return [remote(acc.at[zs[d], span(i, size)], recv_z.at[d, span(i, size)], (s2, r2), (i, d), p)
                for d, p in enumerate(z_ids)]

    def kx(g):
        return [remote(part_kv.at[g, d], recv_kv.at[g, d], (sk, rk), (g, d), p)
                for d, p in enumerate(x_ids)]

    def kz(g):
        return [remote(acc_kv.at[g, zs[d]], recv_kvz.at[g, d], (sj, rj), (g, d), p)
                for d, p in enumerate(z_ids)]

    def zg(i, size):
        here = q_buf.at[x, z, span(i, size)]
        return [remote(here, here, (s3, r3), (i, d), p) for d, p in enumerate(z_ids)]

    def xg(i, size):
        here = q_buf.at[x, :, span(i, size)]
        return [remote(here, here, (s4, r4), (i, d), p) for d, p in enumerate(x_ids)]

    def xl(i, size):
        return [remote(lse.at[xs[d], span(i, size)], lse_recv.at[d, span(i, size)], (s5, r5), (i, d), p)
                for d, p in enumerate(x_ids)]

    def xo(i, size):
        return [remote(o_buf.at[xs[d], span(i, size)], o_recv.at[d, span(i, size)], (s6, r6), (i, d), p)
                for d, p in enumerate(x_ids)]

    def zl(i, size):
        return [remote(mid_lse.at[span(i, size)], mid_lse_recv.at[d, span(i, size)], (s7, r7), (i, d), p)
                for d, p in enumerate(z_ids)]

    def zo(i, size):
        return [remote(mid.at[zs[d], span(i, size)], mid_recv.at[d, span(i, size)], (s8, r8), (i, d), p)
                for d, p in enumerate(z_ids)]

    def za(i, size):
        here = att.at[x, span(i, size), z]
        return [remote(here, here, (s9, r9), (i, d), p) for d, p in enumerate(z_ids)]

    def xa(i, size):
        here = att.at[x, span(i, size)]
        return [remote(here, here, (sa, ra), (i, d), p) for d, p in enumerate(x_ids)]

    def start(copies):
        for copy in copies:
            copy.start()

    def arrive(copies):
        for copy in copies:
            copy.wait_recv()

    def ship(i, size):
        w = w_buf[:, pl.ds(pl.multiple_of(i * dim, dim), size * dim)]
        for d in range(inner - 1):
            out = jnp.dot(hid[xs[d]], w, preferred_element_type=jnp.float32)
            for k in range(size):
                part_x[d, i + k] = out[:, k * dim : (k + 1) * dim]
        start(x1(i, size))
        own = jnp.dot(hid[x], w, preferred_element_type=jnp.float32)
        for k in range(size):
            acc[:, i + k] = own[:, k * dim : (k + 1) * dim].reshape(outer, rows, dim)

    def ship_kv(g):
        ws = [w_kv[:, k, g * dim : (g + 1) * dim] for k in range(2)]
        w = jnp.concatenate(ws, axis=1)
        for d in range(inner - 1):
            part_kv[g, d] = jnp.dot(hid[xs[d]], w, preferred_element_type=jnp.float32)
        start(kx(g))
        own = jnp.dot(hid[x], w, preferred_element_type=jnp.float32)
        acc_kv[g] = own.reshape(outer, rows, 2 * dim)

    def add_x(i, size):
        arrive(x1(i, size))
        for k in range(size):
            total = acc[:, i + k]
            for d in range(inner - 1):
                total += recv_x[d, i + k].reshape(outer, rows, dim)
            acc[:, i + k] = total
        start(z1(i, size))

    def add_z(i, size):
        arrive(z1(i, size))
        for k in range(size):
            total = acc[z, i + k]
            for d in range(outer - 1):
                total += recv_z[d, i + k]
            q_buf[x, z, i + k] = total.astype(jnp.bfloat16)
        start(zg(i, size))

    def add_kv_x(g):
        arrive(kx(g))
        total = acc_kv[g]
        for d in range(inner - 1):
            total += recv_kv[g, d].reshape(outer, rows, 2 * dim)
        acc_kv[g] = total
        start(kz(g))

    def add_kv_z(g):
        arrive(kz(g))
        total = acc_kv[g, z]
        for d in range(outer - 1):
            total += recv_kvz[g, d]
        k_fresh[g, :, :dim] = total[:, :dim].astype(jnp.bfloat16)
        k_fresh[g, :, dim:] = total[:, :dim].astype(jnp.bfloat16)
        turned = total[:, dim:].astype(jnp.bfloat16).astype(jnp.float32).T
        v_fresh[g] = jnp.concatenate(
            [turned, jnp.ones((16, rows), jnp.float32)], axis=0).astype(jnp.bfloat16)

    def spread(i, size):
        arrive(zg(i, size))
        start(xg(i, size))

    def attend(i, size):
        arrive(xg(i, size))
        g = i // group
        augs = []
        for k in range(size):
            q = q_buf[:, :, i + k].reshape(tokens, dim).astype(jnp.float32) * (scale * LOG2E)
            high_q = q.astype(jnp.bfloat16)
            low_q = (q - high_q.astype(jnp.float32)).astype(jnp.bfloat16)
            augs.append(jnp.concatenate([high_q, low_q], axis=1))

        def scores(k, b):
            keys = k_fresh[g] if b < 0 else k_aug[g, b * kb : (b + 1) * kb, :]
            s = lax.dot_general(keys, augs[k], NT, preferred_element_type=jnp.float32)
            return s + hidden_new[...] if b < 0 else s

        order = [(k, b) for b in list(range(slots // kb)) + [-1] for k in range(size)]
        state = [None] * size
        coming = scores(*order[0])
        for n, (k, b) in enumerate(order):
            s = coming
            if n + 1 < len(order):
                coming = scores(*order[n + 1])
            top = jnp.max(s, axis=0, keepdims=True)
            if state[k] is not None:
                top = jnp.maximum(state[k][0], top)
            p = jnp.exp2(s - top).astype(jnp.bfloat16)
            v = v_fresh[g] if b < 0 else v_aug[g, :, b * kb : (b + 1) * kb]
            t = jnp.dot(v, p, preferred_element_type=jnp.float32)
            if state[k] is not None:
                t = t + state[k][1] * jnp.exp2(state[k][0] - top)
            state[k] = (top, t)
        for k in range(size):
            top, total = state[k]
            denom = total[dim : dim + 1, :]
            value = (total[:dim] * (1.0 / denom)).astype(jnp.bfloat16)
            log = top * (1.0 / LOG2E) + jnp.log(denom)
            for v in range(inner):
                o_buf[v, i + k] = value[:, v * half : (v + 1) * half]
                lse[v, i + k] = log[:, v * half : (v + 1) * half]
        start(xl(i, size))
        start(xo(i, size))

    def shares(logs):
        top = functools.reduce(jnp.maximum, logs)
        parts = [jnp.exp(v - top) for v in logs]
        total = sum(parts[1:], parts[0])
        return [w / total for w in parts], top + jnp.log(total)

    def blend_x(i, size):
        arrive(xl(i, size))
        ws, log = shares([lse[x, span(i, size)]] + [lse_recv[d, span(i, size)] for d in range(inner - 1)])
        mid_lse[span(i, size)] = log
        start(zl(i, size))
        arrive(xo(i, size))
        total = ws[0] * o_buf[x, span(i, size)].astype(jnp.float32)
        for d in range(inner - 1):
            total += ws[d + 1] * o_recv[d, span(i, size)].astype(jnp.float32)
        for k in range(size):
            mid[:, i + k] = total[k].reshape(outer, dim // outer, half).astype(jnp.bfloat16)
        start(zo(i, size))

    def blend_z(i, size):
        arrive(zl(i, size))
        ws, _ = shares([mid_lse[span(i, size)]] + [mid_lse_recv[d, span(i, size)] for d in range(outer - 1)])
        arrive(zo(i, size))
        total = ws[0] * mid[z, span(i, size)].astype(jnp.float32)
        for d in range(outer - 1):
            total += ws[d + 1] * mid_recv[d, span(i, size)].astype(jnp.float32)
        total = total.astype(jnp.bfloat16)
        for k in range(size):
            att[x, i + k, z] = total[k]
        start(za(i, size))

    def spread_att(i, size):
        arrive(za(i, size))
        start(xa(i, size))

    def product(i, size, v):
        lhs = att[v, span(i, size)].reshape(size * dim, half).T
        w = wo_buf[pl.ds(pl.multiple_of(i * dim, dim), size * dim), :]
        part[v] += jnp.dot(lhs, w, preferred_element_type=jnp.float32)

    def project_own(i, size):
        product(i, size, x)

    def project_rest(i, size):
        arrive(xa(i, size))
        for v in xs:
            product(i, size, v)

    def prep(g):
        filled = filled_ref[0]
        keep = lax.broadcasted_iota(jnp.int32, (slots, dim), 0) < filled
        keep = jnp.where(keep, 1.0, 0.0).astype(jnp.bfloat16)
        wide = lax.broadcasted_iota(jnp.int32, (16, slots), 1) < filled
        wide = jnp.where(wide, 1.0, 0.0).astype(jnp.bfloat16)
        k_loads[g].wait()
        whole = k_aug[g, :, :dim]
        whole = whole * keep + whole[0:1] * (1.0 - keep)
        k_aug[g, :, :dim] = whole
        k_aug[g, :, dim:] = whole
        v_loads[g].wait()
        v_aug[g, dim:, :] = wide
        v_aug[g, :dim, :] = v_raw[g].T * wide[0:1]

    front = min(FRONT, heads // 2)
    rear = min(REAR, heads // 2)
    wides = (heads - front - rear) // 2
    count = front + wides + rear
    back = front + wides

    def of_block(n, run):
        if isinstance(n, int):
            if n < front:
                run(n, 1)
            elif n < back:
                run(front + 2 * (n - front), 2)
            else:
                run(n + wides, 1)
            return

        if front + rear:
            @pl.when(((n >= 0) & (n < front)) | ((n >= back) & (n < count)))
            def _():
                run(n + (n // back) * wides, 1)

        if wides:
            @pl.when((n >= front) & (n < back))
            def _():
                run(front + 2 * (n - front), 2)

    for b in range(AHEAD):
        of_block(b, ship)
        if b == KV_SHIP[0]:
            kv_load.wait()
            ship_kv(0)
    q_loads[1].wait()
    part[...] = jnp.zeros_like(part)
    places = jnp.broadcast_to(posq_ref[...], (128, tokens)).T
    places_ref[...] = places
    seen = places_ref[pl.ds((x * outer + z) * rows, rows), 0:1] <= posq_ref[...]
    hidden_new[...] = jnp.where(seen, 0.0, HIDE)

    lag = [0]
    for more in (LAG_Z, LAG_ZG, LAG_XG, LAG_XO, LAG_ZO, LAG_ZA, LAG_XA):
        lag.append(lag[-1] + more)

    def step(t, carry):
        def stage(late, run):
            of_block(t - late, run)

        def at(when, run):
            @pl.when(t == when)
            def _():
                run()

        stage(lag[3], attend)
        stage(lag[2], spread)
        stage(lag[1], add_z)
        for g in range(kv_heads):
            last = KV_Z[0] if g == 0 else KV_Z[1] + 2 * (g - 1)
            at(last, functools.partial(add_kv_z, g))
        stage(lag[0], add_x)
        for g in range(kv_heads):
            first = KV_X[0] if g == 0 else KV_X[1] + 2 * (g - 1)
            at(first, functools.partial(add_kv_x, g))

        @pl.when(t + AHEAD < count)
        def _():
            of_block(t + AHEAD, ship)

        for g in range(1, kv_heads):
            at(KV_SHIP[1] + 2 * (g - 1), functools.partial(ship_kv, g))
        stage(lag[4], blend_x)
        stage(lag[5], blend_z)
        stage(lag[6], spread_att)
        for g in range(kv_heads):
            at(PREP + g, functools.partial(prep, g))
        at(lag[6], wo_load.wait)
        stage(lag[6], project_own)
        stage(lag[7], project_rest)
        return carry

    lax.fori_loop(0, count + lag[7], step, 0)

    share = out_ref.shape[0]
    width = part.shape[2]
    whole = part.reshape(others, CORES, share, width)
    for v in range(others):
        core_part[v] = whole[v, 1 - core]
    hop = remote(core_part, core_recv, (sc, rc), 0, twin)
    hop.start()

    def drain(n, carry):
        def run(i, size):
            for kind in [x1, z1, zg, xg, xl, xo, zl, zo, za, xa]:
                for copy in kind(i, size):
                    copy.wait_send()

        of_block(n, run)
        return carry

    hop.wait_recv()
    for d in range(others - 1):
        part_low[d] = (whole[ys[d], core] + core_recv[ys[d]]).astype(jnp.bfloat16)
    last = [remote(part_low.at[d], recv_t.at[d], (st, rt), d, p) for d, p in enumerate(y_ids)]
    start(last)
    lax.fori_loop(0, count, drain, 0)
    for g in range(kv_heads):
        for copy in kx(g) + kz(g):
            copy.wait_send()
    hop.wait_send()
    own = whole[row, core] + core_recv[row]
    for d, copy in enumerate(last):
        copy.wait_recv()
        own += recv_t[d].astype(jnp.float32)
    out_ref[...] = own.astype(out_ref.dtype)
    for copy in last:
        copy.wait_send()


def body(hidden_input, w_query, key_value_weight, w_out, key_value_cache, filled, positions):
    tokens, width = hidden_input.shape
    shards = lax.axis_size("ctx")
    tp_size = lax.axis_size("tp")
    outer, inner = factor(shards)
    rows = tokens // shards
    half = outer * rows
    _, kv_heads, slots, dim = key_value_cache.shape
    heads = w_query.shape[1] // dim
    chunk = dim // outer
    out_width = w_out.shape[1]
    share = tokens // tp_size
    others = tp_size // CORES
    nx, nz, ny = max(inner - 1, 1), max(outer - 1, 1), max(others - 1, 1)
    dma = pltpu.SemaphoreType.DMA
    vmem = pl.BlockSpec(memory_space=pltpu.VMEM)
    hbm = pl.BlockSpec(memory_space=pl.ANY)
    low, full = jnp.bfloat16, jnp.float32
    pairs = []
    for peers in (nx, nz, nz, nx, nx, nx, nz, nz, nz, nx):
        pairs += [dma((heads, peers)), dma((heads, peers))]
    return pl.pallas_call(
        functools.partial(
            layer_kernel, outer, inner, tp_size, kv_heads, dim, 1.0 / math.sqrt(dim),
            math.gcd(slots, 1024),
        ),
        out_shape=jax.ShapeDtypeStruct((share, out_width), low),
        in_specs=[pl.BlockSpec(memory_space=pltpu.SMEM), hbm, vmem, hbm, hbm, hbm, hbm],
        out_specs=vmem,
        scratch_shapes=[
            pltpu.VMEM((inner, half, width), low),
            pltpu.VMEM((width, heads * dim), low),
            pltpu.VMEM(key_value_weight.shape, low),
            pltpu.VMEM((kv_heads, slots, 2 * dim), low),
            pltpu.VMEM((kv_heads, slots, dim), low),
            pltpu.VMEM((kv_heads, dim + 16, slots), low),
            pltpu.VMEM(w_out.shape, low),
            pltpu.VMEM((nx, heads, half, dim), full),
            pltpu.VMEM((nx, heads, half, dim), full),
            pltpu.VMEM((outer, heads, rows, dim), full),
            pltpu.VMEM((nz, heads, rows, dim), full),
            pltpu.VMEM((kv_heads, nx, half, 2 * dim), full),
            pltpu.VMEM((kv_heads, nx, half, 2 * dim), full),
            pltpu.VMEM((kv_heads, outer, rows, 2 * dim), full),
            pltpu.VMEM((kv_heads, nz, rows, 2 * dim), full),
            pltpu.VMEM((kv_heads, rows, 2 * dim), low),
            pltpu.VMEM((kv_heads, dim + 16, rows), low),
            pltpu.VMEM((inner, outer, heads, rows, dim), low),
            pltpu.VMEM((inner, heads, dim, half), low),
            pltpu.VMEM((inner, heads, 1, half), full),
            pltpu.VMEM((nx, heads, dim, half), low),
            pltpu.VMEM((nx, heads, 1, half), full),
            pltpu.VMEM((outer, heads, chunk, half), low),
            pltpu.VMEM((heads, 1, half), full),
            pltpu.VMEM((nz, heads, chunk, half), low),
            pltpu.VMEM((nz, heads, 1, half), full),
            pltpu.VMEM((inner, heads, outer, chunk, half), low),
            pltpu.VMEM((inner, half, out_width), full),
            pltpu.VMEM((others, share, out_width), full),
            pltpu.VMEM((others, share, out_width), full),
            pltpu.VMEM((ny, share, out_width), low),
            pltpu.VMEM((ny, share, out_width), low),
            pltpu.VMEM((tokens, 128), jnp.int32),
            pltpu.VMEM((rows, tokens), full),
            dma(()), dma((3,)), dma((kv_heads,)), dma((kv_heads,)), dma(()),
            *pairs,
            dma((kv_heads, nx)), dma((kv_heads, nx)), dma((kv_heads, nz)), dma((kv_heads, nz)),
            dma((1,)), dma((1,)), dma((ny,)), dma((ny,)),
        ],
        compiler_params=pltpu.CompilerParams(
            collective_id=0, has_side_effects=True, vmem_limit_bytes=60 << 20
        ),
        name="layer",
    )(
        filled, hidden_input.reshape(inner, half, width), positions.reshape(1, tokens),
        w_query, key_value_weight,
        key_value_cache, w_out,
    )


def solution(mesh):
    placed = (
        P(None, "ctx"),
        P("ctx", "tp"),
        P("ctx", None, "tp"),
        P("tp", "ctx"),
        P(None, "tp", "ctx", None),
        P("ctx"),
        P(),
    )
    return jax.shard_map(
        body, mesh=mesh, in_specs=placed, out_specs=P("tp", "ctx"), check_vma=False
    )
```

```python
import functools
import math

import jax
import jax.numpy as jnp
from jax import lax
from jax.experimental import pallas as pl
from jax.experimental.pallas import tpu as pltpu
from jax.sharding import PartitionSpec as P

MESH = pl.DeviceIdType.MESH
HIDE = -1e30
LOG2E = 1.4426950408889634
CORES = 2
PIECES = 2

AHEAD = 2
FRONT = 4
REAR = 2
PREP = 1
KV_SHIP = (1, 5)
LAG_Z = 2
LAG_ZG = 2
LAG_XG = 2
LAG_XO = 2
LAG_ZO = 2
LAG_ZA = 2
LAG_XA = 2
KV_X = (2, 8)
KV_Z = (5, 11)


def factor(shards):
    for inner in (8, 2) if shards > 8 else (2,):
        if shards % inner == 0:
            return shards // inner, inner
    return shards, 1


def peers_of(outer, inner):
    me = lax.axis_index("ctx")
    z = me // inner
    x = me % inner
    xs = [(x + d) % inner for d in range(1, inner)]
    zs = [(z + d) % outer for d in range(1, outer)]
    x_ids = [{"ctx": z * inner + v} for v in xs]
    z_ids = [{"ctx": v * inner + x} for v in zs]
    return x, z, xs, zs, x_ids, z_ids


def remote(src, dst, sems, place, peer):
    return pltpu.make_async_remote_copy(
        src_ref=src,
        dst_ref=dst,
        send_sem=sems[0].at[place],
        recv_sem=sems[1].at[place],
        device_id=peer,
        device_id_type=MESH,
    )


NT = (((1,), (1,)), ((), ()))


def layer_kernel(
    outer, inner, tp_size, kv_heads, dim, scale, kb,
    filled_ref, hid_ref, posq_ref, wq_ref, wkv_ref, cache_ref, wo_ref,
    out_ref,
    hid, w_buf, w_kv, k_aug, v_raw, v_aug, wo_buf,
    part_x, recv_x, acc, recv_z, part_kv, recv_kv, acc_kv, recv_kvz, part_v, recv_v, acc_v, low_v, recv_vz, k_fresh, v_fresh, q_buf,
    o_buf, lse, o_recv, lse_recv, mid, mid_lse, mid_recv, mid_lse_recv, att,
    part, core_part, core_recv, part_low, recv_t, places_ref, hidden_new,
    h_sem, w_sem, k_sem, v_sem, wo_sem,
    s1, r1, s2, r2, s3, r3, s4, r4, s5, r5, s6, r6, s7, r7, s8, r8, s9, r9, sa, ra,
    sk, rk, sj, rj, sc, rc, st, rt,
):
    heads = q_buf.shape[2]
    group = heads // kv_heads
    rows = acc.shape[2]
    half = outer * rows
    tokens = inner * half
    slots = v_raw.shape[1]
    x, z, xs, zs, x_ids, z_ids = peers_of(outer, inner)
    tp = lax.axis_index("tp")
    core = tp % CORES
    row = tp // CORES
    others = tp_size // CORES
    ys = [(row + d) % others for d in range(1, others)]
    y_ids = [{"tp": v * CORES + core} for v in ys]
    twin = {"tp": row * CORES + 1 - core}

    h_load = pltpu.make_async_copy(hid_ref, hid, h_sem)
    q_loads = [pltpu.make_async_copy(
        wq_ref.at[:, pl.ds(p * heads * dim // 2, heads * dim // 2)],
        w_buf.at[:, pl.ds(p * heads * dim // 2, heads * dim // 2)], w_sem.at[p]) for p in range(2)]
    kv_load = pltpu.make_async_copy(wkv_ref, w_kv, w_sem.at[2])
    k_loads = [
        pltpu.make_async_copy(cache_ref.at[0, g], k_aug.at[g, :, pl.ds(0, dim)], k_sem.at[g])
        for g in range(kv_heads)
    ]
    v_loads = [
        pltpu.make_async_copy(cache_ref.at[1, g], v_raw.at[g], v_sem.at[g])
        for g in range(kv_heads)
    ]
    wo_load = pltpu.make_async_copy(wo_ref, wo_buf, wo_sem)
    barrier = pltpu.get_barrier_semaphore()
    friends = x_ids + z_ids + y_ids + [twin]
    for peer in friends:
        pl.semaphore_signal(barrier, inc=1, device_id=peer, device_id_type=MESH)
    for load in [h_load] + q_loads + [kv_load] + k_loads + v_loads + [wo_load]:
        load.start()
    h_load.wait()
    q_loads[0].wait()
    pl.semaphore_wait(barrier, len(friends))

    def span(i, size):
        return pl.ds(i, size)

    def x1(i, size):
        return [remote(part_x.at[d, span(i, size)], recv_x.at[d, span(i, size)], (s1, r1), (i, d), p)
                for d, p in enumerate(x_ids)]

    def z1(i, size):
        return [remote(acc.at[zs[d], span(i, size)], recv_z.at[d, span(i, size)], (s2, r2), (i, d), p)
                for d, p in enumerate(z_ids)]

    def kx(g):
        return [remote(part_kv.at[g, d], recv_kv.at[g, d], (sk, rk), (g, d), p)
                for d, p in enumerate(x_ids)] + [
            remote(part_v.at[g, d], recv_v.at[g, d], (sk, rk), (g, inner + d), p)
            for d, p in enumerate(x_ids)]

    def kz(g):
        return [remote(acc_kv.at[g, zs[d]], recv_kvz.at[g, d], (sj, rj), (g, d), p)
                for d, p in enumerate(z_ids)] + [
            remote(low_v.at[g, zs[d]], recv_vz.at[g, d], (sj, rj), (g, outer + d), p)
            for d, p in enumerate(z_ids)]

    def zg(i, size):
        here = q_buf.at[x, z, span(i, size)]
        return [remote(here, here, (s3, r3), (i, d), p) for d, p in enumerate(z_ids)]

    def xg(i, size):
        here = q_buf.at[x, :, span(i, size)]
        return [remote(here, here, (s4, r4), (i, d), p) for d, p in enumerate(x_ids)]

    def xl(i, size):
        return [remote(lse.at[xs[d], span(i, size)], lse_recv.at[d, span(i, size)], (s5, r5), (i, d), p)
                for d, p in enumerate(x_ids)]

    def xo(i, size):
        return [remote(o_buf.at[xs[d], span(i, size)], o_recv.at[d, span(i, size)], (s6, r6), (i, d), p)
                for d, p in enumerate(x_ids)]

    def zl(i, size):
        return [remote(mid_lse.at[span(i, size)], mid_lse_recv.at[d, span(i, size)], (s7, r7), (i, d), p)
                for d, p in enumerate(z_ids)]

    def zo(i, size):
        return [remote(mid.at[zs[d], span(i, size)], mid_recv.at[d, span(i, size)], (s8, r8), (i, d), p)
                for d, p in enumerate(z_ids)]

    def za(i, size):
        here = att.at[x, span(i, size), z]
        return [remote(here, here, (s9, r9), (i, d), p) for d, p in enumerate(z_ids)]

    def xa(i, size):
        here = att.at[x, span(i, size)]
        return [remote(here, here, (sa, ra), (i, d), p) for d, p in enumerate(x_ids)]

    def start(copies):
        for copy in copies:
            copy.start()

    def arrive(copies):
        for copy in copies:
            copy.wait_recv()

    def ship(i, size):
        w = w_buf[:, pl.ds(pl.multiple_of(i * dim, dim), size * dim)]
        for d in range(inner - 1):
            out = jnp.dot(hid[xs[d]], w, preferred_element_type=jnp.float32)
            for k in range(size):
                part_x[d, i + k] = out[:, k * dim : (k + 1) * dim]
        start(x1(i, size))
        own = jnp.dot(hid[x], w, preferred_element_type=jnp.float32)
        for k in range(size):
            acc[:, i + k] = own[:, k * dim : (k + 1) * dim].reshape(outer, rows, dim)

    def ship_kv(g):
        ws = [w_kv[:, k, g * dim : (g + 1) * dim] for k in range(2)]
        w = jnp.concatenate(ws, axis=1)
        for d in range(inner - 1):
            out = jnp.dot(hid[xs[d]], w, preferred_element_type=jnp.float32)
            part_kv[g, d] = out[:, :dim]
            part_v[g, d] = out[:, dim:].astype(jnp.bfloat16)
        start(kx(g))
        own = jnp.dot(hid[x], w, preferred_element_type=jnp.float32)
        acc_kv[g] = own[:, :dim].reshape(outer, rows, dim)
        acc_v[g] = own[:, dim:].reshape(outer, rows, dim)

    def add_x(i, size):
        arrive(x1(i, size))
        for k in range(size):
            total = acc[:, i + k]
            for d in range(inner - 1):
                total += recv_x[d, i + k].reshape(outer, rows, dim)
            acc[:, i + k] = total
        start(z1(i, size))

    def add_z(i, size):
        arrive(z1(i, size))
        for k in range(size):
            total = acc[z, i + k]
            for d in range(outer - 1):
                total += recv_z[d, i + k]
            q_buf[x, z, i + k] = total.astype(jnp.bfloat16)
        start(zg(i, size))

    def add_kv_x(g):
        arrive(kx(g))
        keys, values = acc_kv[g], acc_v[g]
        for d in range(inner - 1):
            keys += recv_kv[g, d].reshape(outer, rows, dim)
            values += recv_v[g, d].astype(jnp.float32).reshape(outer, rows, dim)
        acc_kv[g] = keys
        acc_v[g] = values
        low_v[g] = values.astype(jnp.bfloat16)
        start(kz(g))

    def add_kv_z(g):
        arrive(kz(g))
        keys, values = acc_kv[g, z], acc_v[g, z]
        for d in range(outer - 1):
            keys += recv_kvz[g, d]
            values += recv_vz[g, d].astype(jnp.float32)
        k_fresh[g, :, :dim] = keys.astype(jnp.bfloat16)
        k_fresh[g, :, dim:] = keys.astype(jnp.bfloat16)
        turned = values.astype(jnp.bfloat16).astype(jnp.float32).T
        v_fresh[g] = jnp.concatenate(
            [turned, jnp.ones((16, rows), jnp.float32)], axis=0).astype(jnp.bfloat16)

    def spread(i, size):
        arrive(zg(i, size))
        start(xg(i, size))

    def attend(i, size):
        arrive(xg(i, size))
        g = i // group
        augs = []
        for k in range(size):
            q = q_buf[:, :, i + k].reshape(tokens, dim).astype(jnp.float32) * (scale * LOG2E)
            high_q = q.astype(jnp.bfloat16)
            low_q = (q - high_q.astype(jnp.float32)).astype(jnp.bfloat16)
            augs.append(jnp.concatenate([high_q, low_q], axis=1))

        def scores(k, b):
            keys = k_fresh[g] if b < 0 else k_aug[g, b * kb : (b + 1) * kb, :]
            s = lax.dot_general(keys, augs[k], NT, preferred_element_type=jnp.float32)
            return s + hidden_new[...] if b < 0 else s

        order = [(k, b) for b in list(range(slots // kb)) + [-1] for k in range(size)]
        state = [None] * size
        coming = scores(*order[0])
        for n, (k, b) in enumerate(order):
            s = coming
            if n + 1 < len(order):
                coming = scores(*order[n + 1])
            top = jnp.max(s, axis=0, keepdims=True)
            if state[k] is not None:
                top = jnp.maximum(state[k][0], top)
            p = jnp.exp2(s - top).astype(jnp.bfloat16)
            v = v_fresh[g] if b < 0 else v_aug[g, :, b * kb : (b + 1) * kb]
            t = jnp.dot(v, p, preferred_element_type=jnp.float32)
            if state[k] is not None:
                t = t + state[k][1] * jnp.exp2(state[k][0] - top)
            state[k] = (top, t)
        for k in range(size):
            top, total = state[k]
            denom = total[dim : dim + 1, :]
            value = (total[:dim] * (1.0 / denom)).astype(jnp.bfloat16)
            log = top * (1.0 / LOG2E) + jnp.log(denom)
            for v in range(inner):
                o_buf[v, i + k] = value[:, v * half : (v + 1) * half]
                lse[v, i + k] = log[:, v * half : (v + 1) * half]
        start(xl(i, size))
        start(xo(i, size))

    def shares(logs):
        top = functools.reduce(jnp.maximum, logs)
        parts = [jnp.exp(v - top) for v in logs]
        total = sum(parts[1:], parts[0])
        return [w / total for w in parts], top + jnp.log(total)

    def blend_x(i, size):
        arrive(xl(i, size))
        ws, log = shares([lse[x, span(i, size)]] + [lse_recv[d, span(i, size)] for d in range(inner - 1)])
        mid_lse[span(i, size)] = log
        start(zl(i, size))
        arrive(xo(i, size))
        total = ws[0] * o_buf[x, span(i, size)].astype(jnp.float32)
        for d in range(inner - 1):
            total += ws[d + 1] * o_recv[d, span(i, size)].astype(jnp.float32)
        for k in range(size):
            mid[:, i + k] = total[k].reshape(outer, dim // outer, half).astype(jnp.bfloat16)
        start(zo(i, size))

    def blend_z(i, size):
        arrive(zl(i, size))
        ws, _ = shares([mid_lse[span(i, size)]] + [mid_lse_recv[d, span(i, size)] for d in range(outer - 1)])
        arrive(zo(i, size))
        total = ws[0] * mid[z, span(i, size)].astype(jnp.float32)
        for d in range(outer - 1):
            total += ws[d + 1] * mid_recv[d, span(i, size)].astype(jnp.float32)
        total = total.astype(jnp.bfloat16)
        for k in range(size):
            att[x, i + k, z] = total[k]
        start(za(i, size))

    def spread_att(i, size):
        arrive(za(i, size))
        start(xa(i, size))

    def product(i, size, v):
        lhs = att[v, span(i, size)].reshape(size * dim, half).T
        w = wo_buf[pl.ds(pl.multiple_of(i * dim, dim), size * dim), :]
        part[v] += jnp.dot(lhs, w, preferred_element_type=jnp.float32)

    def project_own(i, size):
        product(i, size, x)

    def project_rest(i, size):
        arrive(xa(i, size))
        for v in xs:
            product(i, size, v)

    def prep(g):
        filled = filled_ref[0]
        keep = lax.broadcasted_iota(jnp.int32, (slots, dim), 0) < filled
        keep = jnp.where(keep, 1.0, 0.0).astype(jnp.bfloat16)
        wide = lax.broadcasted_iota(jnp.int32, (16, slots), 1) < filled
        wide = jnp.where(wide, 1.0, 0.0).astype(jnp.bfloat16)
        k_loads[g].wait()
        whole = k_aug[g, :, :dim]
        whole = whole * keep + whole[0:1] * (1.0 - keep)
        k_aug[g, :, :dim] = whole
        k_aug[g, :, dim:] = whole
        v_loads[g].wait()
        v_aug[g, dim:, :] = wide
        v_aug[g, :dim, :] = v_raw[g].T * wide[0:1]

    front = min(FRONT, heads // 2)
    rear = min(REAR, heads // 2)
    wides = (heads - front - rear) // 2
    count = front + wides + rear
    back = front + wides

    def of_block(n, run):
        if isinstance(n, int):
            if n < front:
                run(n, 1)
            elif n < back:
                run(front + 2 * (n - front), 2)
            else:
                run(n + wides, 1)
            return

        if front + rear:
            @pl.when(((n >= 0) & (n < front)) | ((n >= back) & (n < count)))
            def _():
                run(n + (n // back) * wides, 1)

        if wides:
            @pl.when((n >= front) & (n < back))
            def _():
                run(front + 2 * (n - front), 2)

    for b in range(AHEAD):
        of_block(b, ship)
        if b == KV_SHIP[0]:
            kv_load.wait()
            ship_kv(0)
    q_loads[1].wait()
    part[...] = jnp.zeros_like(part)
    places = jnp.broadcast_to(posq_ref[...], (128, tokens)).T
    places_ref[...] = places
    seen = places_ref[pl.ds((x * outer + z) * rows, rows), 0:1] <= posq_ref[...]
    hidden_new[...] = jnp.where(seen, 0.0, HIDE)

    lag = [0]
    for more in (LAG_Z, LAG_ZG, LAG_XG, LAG_XO, LAG_ZO, LAG_ZA, LAG_XA):
        lag.append(lag[-1] + more)

    def step(t, carry):
        def stage(late, run):
            of_block(t - late, run)

        def at(when, run):
            @pl.when(t == when)
            def _():
                run()

        stage(lag[3], attend)
        stage(lag[2], spread)
        stage(lag[1], add_z)
        for g in range(kv_heads):
            last = KV_Z[0] if g == 0 else KV_Z[1] + 2 * (g - 1)
            at(last, functools.partial(add_kv_z, g))
        stage(lag[0], add_x)
        for g in range(kv_heads):
            first = KV_X[0] if g == 0 else KV_X[1] + 2 * (g - 1)
            at(first, functools.partial(add_kv_x, g))

        @pl.when(t + AHEAD < count)
        def _():
            of_block(t + AHEAD, ship)

        for g in range(1, kv_heads):
            at(KV_SHIP[1] + 2 * (g - 1), functools.partial(ship_kv, g))
        stage(lag[4], blend_x)
        stage(lag[5], blend_z)
        stage(lag[6], spread_att)
        for g in range(kv_heads):
            at(PREP + g, functools.partial(prep, g))
        at(lag[6], wo_load.wait)
        stage(lag[6], project_own)
        stage(lag[7], project_rest)
        return carry

    lax.fori_loop(0, count + lag[7], step, 0)

    share = out_ref.shape[0]
    width = part.shape[2]
    whole = part.reshape(others, CORES, share, width)
    piece = width // PIECES
    cols = [pl.ds(h * piece, piece) for h in range(PIECES)]
    hops = [remote(core_part.at[h], core_recv.at[h], (sc, rc), h, twin) for h in range(PIECES)]
    for h in range(PIECES):
        for v in range(others):
            core_part[h, v] = whole[v, 1 - core, :, cols[h]]
        hops[h].start()

    def drain(n, carry):
        def run(i, size):
            for kind in [x1, z1, zg, xg, xl, xo, zl, zo, za, xa]:
                for copy in kind(i, size):
                    copy.wait_send()

        of_block(n, run)
        return carry

    last = [[remote(part_low.at[h, d], recv_t.at[h, d], (st, rt), (h, d), p)
             for d, p in enumerate(y_ids)] for h in range(PIECES)]
    for h in range(PIECES):
        hops[h].wait_recv()
        for d in range(others - 1):
            both = whole[ys[d], core, :, cols[h]] + core_recv[h, ys[d]]
            part_low[h, d] = both.astype(jnp.bfloat16)
        start(last[h])
    lax.fori_loop(0, count, drain, 0)
    for g in range(kv_heads):
        for copy in kx(g) + kz(g):
            copy.wait_send()
    for h in range(PIECES):
        hops[h].wait_send()
        own = whole[row, core, :, cols[h]] + core_recv[h, row]
        for d, copy in enumerate(last[h]):
            copy.wait_recv()
            own += recv_t[h, d].astype(jnp.float32)
        out_ref[:, cols[h]] = own.astype(out_ref.dtype)
    for copies in last:
        for copy in copies:
            copy.wait_send()


def body(hidden_input, w_query, key_value_weight, w_out, key_value_cache, filled, positions):
    tokens, width = hidden_input.shape
    shards = lax.axis_size("ctx")
    tp_size = lax.axis_size("tp")
    outer, inner = factor(shards)
    rows = tokens // shards
    half = outer * rows
    _, kv_heads, slots, dim = key_value_cache.shape
    heads = w_query.shape[1] // dim
    chunk = dim // outer
    out_width = w_out.shape[1]
    share = tokens // tp_size
    others = tp_size // CORES
    nx, nz, ny = max(inner - 1, 1), max(outer - 1, 1), max(others - 1, 1)
    dma = pltpu.SemaphoreType.DMA
    vmem = pl.BlockSpec(memory_space=pltpu.VMEM)
    hbm = pl.BlockSpec(memory_space=pl.ANY)
    low, full = jnp.bfloat16, jnp.float32
    pairs = []
    for peers in (nx, nz, nz, nx, nx, nx, nz, nz, nz, nx):
        pairs += [dma((heads, peers)), dma((heads, peers))]
    return pl.pallas_call(
        functools.partial(
            layer_kernel, outer, inner, tp_size, kv_heads, dim, 1.0 / math.sqrt(dim),
            math.gcd(slots, 1024),
        ),
        out_shape=jax.ShapeDtypeStruct((share, out_width), low),
        in_specs=[pl.BlockSpec(memory_space=pltpu.SMEM), hbm, vmem, hbm, hbm, hbm, hbm],
        out_specs=vmem,
        scratch_shapes=[
            pltpu.VMEM((inner, half, width), low),
            pltpu.VMEM((width, heads * dim), low),
            pltpu.VMEM(key_value_weight.shape, low),
            pltpu.VMEM((kv_heads, slots, 2 * dim), low),
            pltpu.VMEM((kv_heads, slots, dim), low),
            pltpu.VMEM((kv_heads, dim + 16, slots), low),
            pltpu.VMEM(w_out.shape, low),
            pltpu.VMEM((nx, heads, half, dim), full),
            pltpu.VMEM((nx, heads, half, dim), full),
            pltpu.VMEM((outer, heads, rows, dim), full),
            pltpu.VMEM((nz, heads, rows, dim), full),
            pltpu.VMEM((kv_heads, nx, half, dim), full),
            pltpu.VMEM((kv_heads, nx, half, dim), full),
            pltpu.VMEM((kv_heads, outer, rows, dim), full),
            pltpu.VMEM((kv_heads, nz, rows, dim), full),
            pltpu.VMEM((kv_heads, nx, half, dim), low),
            pltpu.VMEM((kv_heads, nx, half, dim), low),
            pltpu.VMEM((kv_heads, outer, rows, dim), full),
            pltpu.VMEM((kv_heads, outer, rows, dim), low),
            pltpu.VMEM((kv_heads, nz, rows, dim), low),
            pltpu.VMEM((kv_heads, rows, 2 * dim), low),
            pltpu.VMEM((kv_heads, dim + 16, rows), low),
            pltpu.VMEM((inner, outer, heads, rows, dim), low),
            pltpu.VMEM((inner, heads, dim, half), low),
            pltpu.VMEM((inner, heads, 1, half), full),
            pltpu.VMEM((nx, heads, dim, half), low),
            pltpu.VMEM((nx, heads, 1, half), full),
            pltpu.VMEM((outer, heads, chunk, half), low),
            pltpu.VMEM((heads, 1, half), full),
            pltpu.VMEM((nz, heads, chunk, half), low),
            pltpu.VMEM((nz, heads, 1, half), full),
            pltpu.VMEM((inner, heads, outer, chunk, half), low),
            pltpu.VMEM((inner, half, out_width), full),
            pltpu.VMEM((PIECES, others, share, out_width // PIECES), full),
            pltpu.VMEM((PIECES, others, share, out_width // PIECES), full),
            pltpu.VMEM((PIECES, ny, share, out_width // PIECES), low),
            pltpu.VMEM((PIECES, ny, share, out_width // PIECES), low),
            pltpu.VMEM((tokens, 128), jnp.int32),
            pltpu.VMEM((rows, tokens), full),
            dma(()), dma((3,)), dma((kv_heads,)), dma((kv_heads,)), dma(()),
            *pairs,
            dma((kv_heads, 2 * inner)), dma((kv_heads, 2 * inner)),
            dma((kv_heads, 2 * outer)), dma((kv_heads, 2 * outer)),
            dma((PIECES,)), dma((PIECES,)), dma((PIECES, ny)), dma((PIECES, ny)),
        ],
        compiler_params=pltpu.CompilerParams(
            collective_id=0, has_side_effects=True, vmem_limit_bytes=60 << 20
        ),
        name="layer",
    )(
        filled, hidden_input.reshape(inner, half, width), positions.reshape(1, tokens),
        w_query, key_value_weight,
        key_value_cache, w_out,
    )


def solution(mesh):
    placed = (
        P(None, "ctx"),
        P("ctx", "tp"),
        P("ctx", None, "tp"),
        P("tp", "ctx"),
        P(None, "tp", "ctx", None),
        P("ctx"),
        P(),
    )
    return jax.shard_map(
        body, mesh=mesh, in_specs=placed, out_specs=P("tp", "ctx"), check_vma=False
    )
```

```python
import functools
import math

import jax
import jax.numpy as jnp
from jax import lax
from jax.experimental import pallas as pl
from jax.experimental.pallas import tpu as pltpu
from jax.sharding import PartitionSpec as P

MESH = pl.DeviceIdType.MESH
HIDE = -1e30
LOG2E = 1.4426950408889634
CORES = 2
PIECES = 2

AHEAD = 2
FRONT = 4
REAR = 2
PREP = 1
KV_SHIP = (1, 6)
LAG_Z = 2
LAG_ZG = 2
LAG_XG = 2
LAG_XO = 2
LAG_ZO = 2
LAG_ZA = 2
LAG_XA = 2
KV_X = (2, 9)
KV_Z = (5, 11)


def factor(shards):
    for inner in (8, 2) if shards > 8 else (2,):
        if shards % inner == 0:
            return shards // inner, inner
    return shards, 1


def peers_of(outer, inner):
    me = lax.axis_index("ctx")
    z = me // inner
    x = me % inner
    xs = [(x + d) % inner for d in range(1, inner)]
    zs = [(z + d) % outer for d in range(1, outer)]
    x_ids = [{"ctx": z * inner + v} for v in xs]
    z_ids = [{"ctx": v * inner + x} for v in zs]
    return x, z, xs, zs, x_ids, z_ids


def remote(src, dst, sems, place, peer):
    return pltpu.make_async_remote_copy(
        src_ref=src,
        dst_ref=dst,
        send_sem=sems[0].at[place],
        recv_sem=sems[1].at[place],
        device_id=peer,
        device_id_type=MESH,
    )


NT = (((1,), (1,)), ((), ()))


def layer_kernel(
    outer, inner, tp_size, kv_heads, dim, scale, kb,
    filled_ref, hid_ref, posq_ref, wq_ref, wkv_ref, cache_ref, wo_ref,
    out_ref,
    hid, w_buf, w_kv, k_aug, v_raw, v_aug, wo_buf,
    part_x, recv_x, acc, recv_z, part_kv, recv_kv, acc_kv, recv_kvz, part_v, recv_v, acc_v, low_v, recv_vz, k_fresh, v_fresh, q_buf,
    o_buf, lse, o_recv, lse_recv, mid, mid_lse, mid_recv, mid_lse_recv, att,
    part, core_part, core_recv, part_low, recv_t, places_ref, hidden_new,
    h_sem, w_sem, k_sem, v_sem, wo_sem,
    s1, r1, s2, r2, s3, r3, s4, r4, s5, r5, s6, r6, s7, r7, s8, r8, s9, r9, sa, ra,
    sk, rk, sj, rj, sc, rc, st, rt,
):
    heads = q_buf.shape[2]
    group = heads // kv_heads
    rows = acc.shape[2]
    half = outer * rows
    tokens = inner * half
    slots = v_raw.shape[1]
    x, z, xs, zs, x_ids, z_ids = peers_of(outer, inner)
    tp = lax.axis_index("tp")
    core = tp % CORES
    row = tp // CORES
    others = tp_size // CORES
    ys = [(row + d) % others for d in range(1, others)]
    y_ids = [{"tp": v * CORES + core} for v in ys]
    twin = {"tp": row * CORES + 1 - core}

    h_load = pltpu.make_async_copy(hid_ref, hid, h_sem)
    q_loads = [pltpu.make_async_copy(
        wq_ref.at[:, pl.ds(p * heads * dim // 2, heads * dim // 2)],
        w_buf.at[:, pl.ds(p * heads * dim // 2, heads * dim // 2)], w_sem.at[p]) for p in range(2)]
    kv_load = pltpu.make_async_copy(wkv_ref, w_kv, w_sem.at[2])
    k_loads = [
        pltpu.make_async_copy(cache_ref.at[0, g], k_aug.at[g, :, pl.ds(0, dim)], k_sem.at[g])
        for g in range(kv_heads)
    ]
    v_loads = [
        pltpu.make_async_copy(cache_ref.at[1, g], v_raw.at[g], v_sem.at[g])
        for g in range(kv_heads)
    ]
    wo_load = pltpu.make_async_copy(wo_ref, wo_buf, wo_sem)
    barrier = pltpu.get_barrier_semaphore()
    friends = x_ids + z_ids + y_ids + [twin]
    for peer in friends:
        pl.semaphore_signal(barrier, inc=1, device_id=peer, device_id_type=MESH)
    for load in [h_load] + q_loads + [kv_load] + k_loads + v_loads + [wo_load]:
        load.start()
    h_load.wait()
    q_loads[0].wait()
    pl.semaphore_wait(barrier, len(friends))

    def span(i, size):
        return pl.ds(i, size)

    def x1(i, size):
        return [remote(part_x.at[d, span(i, size)], recv_x.at[d, span(i, size)], (s1, r1), (i, d), p)
                for d, p in enumerate(x_ids)]

    def z1(i, size):
        return [remote(acc.at[zs[d], span(i, size)], recv_z.at[d, span(i, size)], (s2, r2), (i, d), p)
                for d, p in enumerate(z_ids)]

    def kx(g):
        return [remote(part_kv.at[g, d], recv_kv.at[g, d], (sk, rk), (g, d), p)
                for d, p in enumerate(x_ids)] + [
            remote(part_v.at[g, d], recv_v.at[g, d], (sk, rk), (g, inner + d), p)
            for d, p in enumerate(x_ids)]

    def kz(g):
        return [remote(acc_kv.at[g, zs[d]], recv_kvz.at[g, d], (sj, rj), (g, d), p)
                for d, p in enumerate(z_ids)] + [
            remote(low_v.at[g, zs[d]], recv_vz.at[g, d], (sj, rj), (g, outer + d), p)
            for d, p in enumerate(z_ids)]

    def zg(i, size):
        here = q_buf.at[x, z, span(i, size)]
        return [remote(here, here, (s3, r3), (i, d), p) for d, p in enumerate(z_ids)]

    def xg(i, size):
        here = q_buf.at[x, :, span(i, size)]
        return [remote(here, here, (s4, r4), (i, d), p) for d, p in enumerate(x_ids)]

    def xl(i, size):
        return [remote(lse.at[xs[d], span(i, size)], lse_recv.at[d, span(i, size)], (s5, r5), (i, d), p)
                for d, p in enumerate(x_ids)]

    def xo(i, size):
        return [remote(o_buf.at[xs[d], span(i, size)], o_recv.at[d, span(i, size)], (s6, r6), (i, d), p)
                for d, p in enumerate(x_ids)]

    def zl(i, size):
        return [remote(mid_lse.at[span(i, size)], mid_lse_recv.at[d, span(i, size)], (s7, r7), (i, d), p)
                for d, p in enumerate(z_ids)]

    def zo(i, size):
        return [remote(mid.at[zs[d], span(i, size)], mid_recv.at[d, span(i, size)], (s8, r8), (i, d), p)
                for d, p in enumerate(z_ids)]

    def za(i, size):
        here = att.at[x, span(i, size), z]
        return [remote(here, here, (s9, r9), (i, d), p) for d, p in enumerate(z_ids)]

    def xa(i, size):
        here = att.at[x, span(i, size)]
        return [remote(here, here, (sa, ra), (i, d), p) for d, p in enumerate(x_ids)]

    def start(copies):
        for copy in copies:
            copy.start()

    def arrive(copies):
        for copy in copies:
            copy.wait_recv()

    def ship(i, size):
        w = w_buf[:, pl.ds(pl.multiple_of(i * dim, dim), size * dim)]
        for d in range(inner - 1):
            out = jnp.dot(hid[xs[d]], w, preferred_element_type=jnp.float32)
            for k in range(size):
                part_x[d, i + k] = out[:, k * dim : (k + 1) * dim]
        start(x1(i, size))
        own = jnp.dot(hid[x], w, preferred_element_type=jnp.float32)
        for k in range(size):
            acc[:, i + k] = own[:, k * dim : (k + 1) * dim].reshape(outer, rows, dim)

    def ship_kv(g):
        ws = [w_kv[:, k, g * dim : (g + 1) * dim] for k in range(2)]
        w = jnp.concatenate(ws, axis=1)
        for d in range(inner - 1):
            out = jnp.dot(hid[xs[d]], w, preferred_element_type=jnp.float32)
            part_kv[g, d] = out[:, :dim]
            part_v[g, d] = out[:, dim:].astype(jnp.bfloat16)
        start(kx(g))
        own = jnp.dot(hid[x], w, preferred_element_type=jnp.float32)
        acc_kv[g] = own[:, :dim].reshape(outer, rows, dim)
        acc_v[g] = own[:, dim:].reshape(outer, rows, dim)

    def add_x(i, size):
        arrive(x1(i, size))
        for k in range(size):
            total = acc[:, i + k]
            for d in range(inner - 1):
                total += recv_x[d, i + k].reshape(outer, rows, dim)
            acc[:, i + k] = total
        start(z1(i, size))

    def add_z(i, size):
        arrive(z1(i, size))
        for k in range(size):
            total = acc[z, i + k]
            for d in range(outer - 1):
                total += recv_z[d, i + k]
            q_buf[x, z, i + k] = total.astype(jnp.bfloat16)
        start(zg(i, size))

    def add_kv_x(g):
        arrive(kx(g))
        keys, values = acc_kv[g], acc_v[g]
        for d in range(inner - 1):
            keys += recv_kv[g, d].reshape(outer, rows, dim)
            values += recv_v[g, d].astype(jnp.float32).reshape(outer, rows, dim)
        acc_kv[g] = keys
        acc_v[g] = values
        low_v[g] = values.astype(jnp.bfloat16)
        start(kz(g))

    def add_kv_z(g):
        arrive(kz(g))
        keys, values = acc_kv[g, z], acc_v[g, z]
        for d in range(outer - 1):
            keys += recv_kvz[g, d]
            values += recv_vz[g, d].astype(jnp.float32)
        k_fresh[g, :, :dim] = keys.astype(jnp.bfloat16)
        k_fresh[g, :, dim:] = keys.astype(jnp.bfloat16)
        turned = values.astype(jnp.bfloat16).astype(jnp.float32).T
        v_fresh[g] = jnp.concatenate(
            [turned, jnp.ones((16, rows), jnp.float32)], axis=0).astype(jnp.bfloat16)

    def spread(i, size):
        arrive(zg(i, size))
        start(xg(i, size))

    def attend(i, size):
        arrive(xg(i, size))
        g = i // group
        augs = []
        for k in range(size):
            q = q_buf[:, :, i + k].reshape(tokens, dim).astype(jnp.float32) * (scale * LOG2E)
            high_q = q.astype(jnp.bfloat16)
            low_q = (q - high_q.astype(jnp.float32)).astype(jnp.bfloat16)
            augs.append(jnp.concatenate([high_q, low_q], axis=1))

        def scores(k, b):
            keys = k_fresh[g] if b < 0 else k_aug[g, b * kb : (b + 1) * kb, :]
            s = lax.dot_general(keys, augs[k], NT, preferred_element_type=jnp.float32)
            return s + hidden_new[...] if b < 0 else s

        order = [(k, b) for b in list(range(slots // kb)) + [-1] for k in range(size)]
        state = [None] * size
        coming = scores(*order[0])
        for n, (k, b) in enumerate(order):
            s = coming
            if n + 1 < len(order):
                coming = scores(*order[n + 1])
            top = jnp.max(s, axis=0, keepdims=True)
            if state[k] is not None:
                top = jnp.maximum(state[k][0], top)
            p = jnp.exp2(s - top).astype(jnp.bfloat16)
            v = v_fresh[g] if b < 0 else v_aug[g, :, b * kb : (b + 1) * kb]
            t = jnp.dot(v, p, preferred_element_type=jnp.float32)
            if state[k] is not None:
                t = t + state[k][1] * jnp.exp2(state[k][0] - top)
            state[k] = (top, t)
        for k in range(size):
            top, total = state[k]
            denom = total[dim : dim + 1, :]
            value = (total[:dim] * (1.0 / denom)).astype(jnp.bfloat16)
            log = top * (1.0 / LOG2E) + jnp.log(denom)
            for v in range(inner):
                o_buf[v, i + k] = value[:, v * half : (v + 1) * half]
                lse[v, i + k] = log[:, v * half : (v + 1) * half]
        start(xl(i, size))
        start(xo(i, size))

    def shares(logs):
        top = functools.reduce(jnp.maximum, logs)
        parts = [jnp.exp(v - top) for v in logs]
        total = sum(parts[1:], parts[0])
        return [w / total for w in parts], top + jnp.log(total)

    def blend_x(i, size):
        arrive(xl(i, size))
        ws, log = shares([lse[x, span(i, size)]] + [lse_recv[d, span(i, size)] for d in range(inner - 1)])
        mid_lse[span(i, size)] = log
        start(zl(i, size))
        arrive(xo(i, size))
        total = ws[0] * o_buf[x, span(i, size)].astype(jnp.float32)
        for d in range(inner - 1):
            total += ws[d + 1] * o_recv[d, span(i, size)].astype(jnp.float32)
        for k in range(size):
            mid[:, i + k] = total[k].reshape(outer, dim // outer, half).astype(jnp.bfloat16)
        start(zo(i, size))

    def blend_z(i, size):
        arrive(zl(i, size))
        ws, _ = shares([mid_lse[span(i, size)]] + [mid_lse_recv[d, span(i, size)] for d in range(outer - 1)])
        arrive(zo(i, size))
        total = ws[0] * mid[z, span(i, size)].astype(jnp.float32)
        for d in range(outer - 1):
            total += ws[d + 1] * mid_recv[d, span(i, size)].astype(jnp.float32)
        total = total.astype(jnp.bfloat16)
        for k in range(size):
            att[x, i + k, z] = total[k]
        start(za(i, size))

    def spread_att(i, size):
        arrive(za(i, size))
        start(xa(i, size))

    def product(i, size, v):
        lhs = att[v, span(i, size)].reshape(size * dim, half).T
        w = wo_buf[pl.ds(pl.multiple_of(i * dim, dim), size * dim), :]
        part[v] += jnp.dot(lhs, w, preferred_element_type=jnp.float32)

    def project_own(i, size):
        product(i, size, x)

    def project_rest(i, size):
        arrive(xa(i, size))
        for v in xs:
            product(i, size, v)

    def prep(g):
        filled = filled_ref[0]
        keep = lax.broadcasted_iota(jnp.int32, (slots, dim), 0) < filled
        keep = jnp.where(keep, 1.0, 0.0).astype(jnp.bfloat16)
        wide = lax.broadcasted_iota(jnp.int32, (16, slots), 1) < filled
        wide = jnp.where(wide, 1.0, 0.0).astype(jnp.bfloat16)
        k_loads[g].wait()
        whole = k_aug[g, :, :dim]
        whole = whole * keep + whole[0:1] * (1.0 - keep)
        k_aug[g, :, :dim] = whole
        k_aug[g, :, dim:] = whole
        v_loads[g].wait()
        v_aug[g, dim:, :] = wide
        v_aug[g, :dim, :] = v_raw[g].T * wide[0:1]

    front = min(FRONT, heads // 2)
    rear = min(REAR, heads // 2)
    wides = (heads - front - rear) // 2
    count = front + wides + rear
    back = front + wides

    def of_block(n, run):
        if isinstance(n, int):
            if n < front:
                run(n, 1)
            elif n < back:
                run(front + 2 * (n - front), 2)
            else:
                run(n + wides, 1)
            return

        if front + rear:
            @pl.when(((n >= 0) & (n < front)) | ((n >= back) & (n < count)))
            def _():
                run(n + (n // back) * wides, 1)

        if wides:
            @pl.when((n >= front) & (n < back))
            def _():
                run(front + 2 * (n - front), 2)

    for b in range(AHEAD):
        of_block(b, ship)
        if b == KV_SHIP[0]:
            kv_load.wait()
            ship_kv(0)
    q_loads[1].wait()
    part[...] = jnp.zeros_like(part)
    places = jnp.broadcast_to(posq_ref[...], (128, tokens)).T
    places_ref[...] = places
    seen = places_ref[pl.ds((x * outer + z) * rows, rows), 0:1] <= posq_ref[...]
    hidden_new[...] = jnp.where(seen, 0.0, HIDE)

    lag = [0]
    for more in (LAG_Z, LAG_ZG, LAG_XG, LAG_XO, LAG_ZO, LAG_ZA, LAG_XA):
        lag.append(lag[-1] + more)

    def step(t, carry):
        def stage(late, run):
            of_block(t - late, run)

        def at(when, run):
            @pl.when(t == when)
            def _():
                run()

        stage(lag[3], attend)
        stage(lag[2], spread)
        stage(lag[1], add_z)
        for g in range(kv_heads):
            last = KV_Z[0] if g == 0 else KV_Z[1] + 2 * (g - 1)
            at(last, functools.partial(add_kv_z, g))
        stage(lag[0], add_x)
        for g in range(kv_heads):
            first = KV_X[0] if g == 0 else KV_X[1] + 2 * (g - 1)
            at(first, functools.partial(add_kv_x, g))

        @pl.when(t + AHEAD < count)
        def _():
            of_block(t + AHEAD, ship)

        for g in range(1, kv_heads):
            at(KV_SHIP[1] + 2 * (g - 1), functools.partial(ship_kv, g))
        stage(lag[4], blend_x)
        stage(lag[5], blend_z)
        stage(lag[6], spread_att)
        for g in range(kv_heads):
            at(PREP + g, functools.partial(prep, g))
        at(lag[6], wo_load.wait)
        stage(lag[6], project_own)
        stage(lag[7], project_rest)
        return carry

    lax.fori_loop(0, count + lag[7], step, 0)

    share = out_ref.shape[0]
    width = part.shape[2]
    whole = part.reshape(others, CORES, share, width)
    piece = width // PIECES
    cols = [pl.ds(h * piece, piece) for h in range(PIECES)]
    hops = [remote(core_part.at[h], core_recv.at[h], (sc, rc), h, twin) for h in range(PIECES)]
    for h in range(PIECES):
        for v in range(others):
            core_part[h, v] = whole[v, 1 - core, :, cols[h]]
        hops[h].start()

    def drain(n, carry):
        def run(i, size):
            for kind in [x1, z1, zg, xg, xl, xo, zl, zo, za, xa]:
                for copy in kind(i, size):
                    copy.wait_send()

        of_block(n, run)
        return carry

    last = [[remote(part_low.at[h, d], recv_t.at[h, d], (st, rt), (h, d), p)
             for d, p in enumerate(y_ids)] for h in range(PIECES)]
    for h in range(PIECES):
        hops[h].wait_recv()
        for d in range(others - 1):
            both = whole[ys[d], core, :, cols[h]] + core_recv[h, ys[d]]
            part_low[h, d] = both.astype(jnp.bfloat16)
        start(last[h])
    lax.fori_loop(0, count, drain, 0)
    for g in range(kv_heads):
        for copy in kx(g) + kz(g):
            copy.wait_send()
    for h in range(PIECES):
        hops[h].wait_send()
        own = whole[row, core, :, cols[h]] + core_recv[h, row]
        for d, copy in enumerate(last[h]):
            copy.wait_recv()
            own += recv_t[h, d].astype(jnp.float32)
        out_ref[:, cols[h]] = own.astype(out_ref.dtype)
    for copies in last:
        for copy in copies:
            copy.wait_send()


def body(hidden_input, w_query, key_value_weight, w_out, key_value_cache, filled, positions):
    tokens, width = hidden_input.shape
    shards = lax.axis_size("ctx")
    tp_size = lax.axis_size("tp")
    outer, inner = factor(shards)
    rows = tokens // shards
    half = outer * rows
    _, kv_heads, slots, dim = key_value_cache.shape
    heads = w_query.shape[1] // dim
    chunk = dim // outer
    out_width = w_out.shape[1]
    share = tokens // tp_size
    others = tp_size // CORES
    nx, nz, ny = max(inner - 1, 1), max(outer - 1, 1), max(others - 1, 1)
    dma = pltpu.SemaphoreType.DMA
    vmem = pl.BlockSpec(memory_space=pltpu.VMEM)
    hbm = pl.BlockSpec(memory_space=pl.ANY)
    low, full = jnp.bfloat16, jnp.float32
    pairs = []
    for peers in (nx, nz, nz, nx, nx, nx, nz, nz, nz, nx):
        pairs += [dma((heads, peers)), dma((heads, peers))]
    return pl.pallas_call(
        functools.partial(
            layer_kernel, outer, inner, tp_size, kv_heads, dim, 1.0 / math.sqrt(dim),
            math.gcd(slots, 2048),
        ),
        out_shape=jax.ShapeDtypeStruct((share, out_width), low),
        in_specs=[pl.BlockSpec(memory_space=pltpu.SMEM), hbm, vmem, hbm, hbm, hbm, hbm],
        out_specs=vmem,
        scratch_shapes=[
            pltpu.VMEM((inner, half, width), low),
            pltpu.VMEM((width, heads * dim), low),
            pltpu.VMEM(key_value_weight.shape, low),
            pltpu.VMEM((kv_heads, slots, 2 * dim), low),
            pltpu.VMEM((kv_heads, slots, dim), low),
            pltpu.VMEM((kv_heads, dim + 16, slots), low),
            pltpu.VMEM(w_out.shape, low),
            pltpu.VMEM((nx, heads, half, dim), full),
            pltpu.VMEM((nx, heads, half, dim), full),
            pltpu.VMEM((outer, heads, rows, dim), full),
            pltpu.VMEM((nz, heads, rows, dim), full),
            pltpu.VMEM((kv_heads, nx, half, dim), full),
            pltpu.VMEM((kv_heads, nx, half, dim), full),
            pltpu.VMEM((kv_heads, outer, rows, dim), full),
            pltpu.VMEM((kv_heads, nz, rows, dim), full),
            pltpu.VMEM((kv_heads, nx, half, dim), low),
            pltpu.VMEM((kv_heads, nx, half, dim), low),
            pltpu.VMEM((kv_heads, outer, rows, dim), full),
            pltpu.VMEM((kv_heads, outer, rows, dim), low),
            pltpu.VMEM((kv_heads, nz, rows, dim), low),
            pltpu.VMEM((kv_heads, rows, 2 * dim), low),
            pltpu.VMEM((kv_heads, dim + 16, rows), low),
            pltpu.VMEM((inner, outer, heads, rows, dim), low),
            pltpu.VMEM((inner, heads, dim, half), low),
            pltpu.VMEM((inner, heads, 1, half), full),
            pltpu.VMEM((nx, heads, dim, half), low),
            pltpu.VMEM((nx, heads, 1, half), full),
            pltpu.VMEM((outer, heads, chunk, half), low),
            pltpu.VMEM((heads, 1, half), full),
            pltpu.VMEM((nz, heads, chunk, half), low),
            pltpu.VMEM((nz, heads, 1, half), full),
            pltpu.VMEM((inner, heads, outer, chunk, half), low),
            pltpu.VMEM((inner, half, out_width), full),
            pltpu.VMEM((PIECES, others, share, out_width // PIECES), full),
            pltpu.VMEM((PIECES, others, share, out_width // PIECES), full),
            pltpu.VMEM((PIECES, ny, share, out_width // PIECES), low),
            pltpu.VMEM((PIECES, ny, share, out_width // PIECES), low),
            pltpu.VMEM((tokens, 128), jnp.int32),
            pltpu.VMEM((rows, tokens), full),
            dma(()), dma((3,)), dma((kv_heads,)), dma((kv_heads,)), dma(()),
            *pairs,
            dma((kv_heads, 2 * inner)), dma((kv_heads, 2 * inner)),
            dma((kv_heads, 2 * outer)), dma((kv_heads, 2 * outer)),
            dma((PIECES,)), dma((PIECES,)), dma((PIECES, ny)), dma((PIECES, ny)),
        ],
        compiler_params=pltpu.CompilerParams(
            collective_id=0, has_side_effects=True, vmem_limit_bytes=60 << 20
        ),
        name="layer",
    )(
        filled, hidden_input.reshape(inner, half, width), positions.reshape(1, tokens),
        w_query, key_value_weight,
        key_value_cache, w_out,
    )


def solution(mesh):
    placed = (
        P(None, "ctx"),
        P("ctx", "tp"),
        P("ctx", None, "tp"),
        P("tp", "ctx"),
        P(None, "tp", "ctx", None),
        P("ctx"),
        P(),
    )
    return jax.shard_map(
        body, mesh=mesh, in_specs=placed, out_specs=P("tp", "ctx"), check_vma=False
    )
```
